32 devices in a mesh: freq: 2 (over x), tile: 16 (over z, y, core).
Axes of the slice: x: 2, y: 2, z: 4, core: 2. Of those that a mesh axis runs over, the one named last changes fastest.
Arguments:
- model_start: float32 [2, 4096, 128], P('freq', 'tile'), may hold values from -6 to 6
- data: bfloat16 [2, 4096, 128], P('freq', 'tile'), may hold values from -6 to 6
- col_factors: bfloat16 [2, 128, 2, 112, 256], P('freq', 'tile'), may hold values from -0.375 to 0.375
- row_factors: bfloat16 [2, 128, 2, 112, 256], P('freq', 'tile'), may hold values from -0.1875 to 0.1875
- ranks: int32 [2, 16, 8], P('freq'), may hold values from 16 to 112
- gate_window: int32 [64, 2], replicated, may hold values from 0 to 2047, as said below
- step_sizes: float32 [2], P('freq'), may hold values from 0.2 to 0.6
Outputs:
- model_final: float32 [2, 4096, 128], P('freq', 'tile')
The draws below stay inside these ranges and needn't reach their ends.
Inputs may be any that keep to these rules, and one draw needn't show every extreme that they name: `gate_window`: each row is (start, end) with 256 <= end - start <= 1024.
All inputs are finite; a program needn't handle non-finite values.
Results may differ from the reference program's by a relative error of at most 0.0085.
Values may be sent and summed in bfloat16 or wider, within the bound.
A program may use at most 64 MiB of HBM per device.

```python
import math
import jax
import jax.numpy as jnp
from jax import lax

B = 256
RMAX = 112
RMIN = 16
TPD = 8
NV = 64
NT = 2048
ITERS = 2
FREQS = 2
NS = 4096
NR = 4096
SLOTS = 128
N_TILE = 16


def draw_gate_window(key, part):
    first, second = jax.random.split(jax.random.fold_in(key, 23), 2)
    opening = jax.random.randint(first, (NV,), 0, NT // 2, dtype=jnp.int32)
    length = jax.random.randint(second, (NV,), NT // 8, NT // 2 + 1, dtype=jnp.int32)
    return jnp.stack([opening, opening + length], axis=-1).astype(jnp.int32)


def touch_ends(entries, own_key, smallest, largest):
    longest = entries.shape.index(max(entries.shape))
    spots = []
    for shift in (0, 1):
        where = [jax.random.randint(jax.random.fold_in(own_key, axis), (), 0, length) for axis, length in enumerate(entries.shape)]
        where[longest] = (where[longest] + shift) % entries.shape[longest]
        spots.append(tuple(where))
    return entries.at[spots[0]].set(smallest).at[spots[1]].set(largest)


def block_scale(rng, dims, shards, smallest, top_value):
    gain = 1.0
    for position, parts in shards:
        heights = jax.random.uniform(jax.random.fold_in(jax.random.fold_in(rng, 6), position), (parts,), jnp.float32, smallest / len(shards), top_value / len(shards))
        gain = gain * jnp.repeat(jnp.exp(heights), dims[position] // parts).reshape((-1,) + (1,) * (len(dims) - 1 - position))
    return gain


def normal_values(stream_key, extent, deviation, reach, cuts=(), kind=jnp.bfloat16):
    drawn = jax.random.normal(stream_key, extent, jnp.float32) * deviation
    if len(cuts) > 0:
        drawn = block_scale(stream_key, extent, cuts, -0.22, 0.18) * drawn
    return jnp.clip(drawn, min=-reach, max=reach).astype(kind)


def setup_inputs(seed: int = 0) -> dict:
    keys = jax.random.split(jax.random.key(seed), 8)
    return {
        "model_start": normal_values(keys[0], (FREQS, NS, 2 * NV), 1.0, 6.0, ((0, 2), (1, 16)), jnp.float32),
        "data": normal_values(keys[1], (FREQS, NR, 2 * NV), 1.0, 6.0, ((0, 2), (1, 16))),
        "col_factors": normal_values(keys[2], (FREQS, SLOTS, 2, RMAX, B), B ** -0.5, 0.375, ((0, 2), (1, 16))),
        "row_factors": normal_values(keys[3], (FREQS, SLOTS, 2, RMAX, B), (TPD * RMAX) ** -0.5, 0.1875, ((0, 2), (1, 16))),
        "ranks": touch_ends(jax.random.randint(keys[4], (FREQS, N_TILE, TPD), RMIN, RMAX + 1), jax.random.fold_in(keys[4], 1), RMIN, RMAX).astype(jnp.int32),
        "gate_window": draw_gate_window(jax.random.fold_in(keys[7], 71), 0),
        "step_sizes": jnp.clip(jnp.exp(math.log(0.6) - 1.0986123 * jax.random.uniform(keys[6], (FREQS,), jnp.float32) ** block_scale(keys[6], (FREQS,), ((0, 2),), -0.2, 0.2)), 0.2, 0.6),
    }


def rotate(z):
    half = z.shape[-1] // 2
    return jnp.concatenate([-z[..., half:], z[..., :half]], axis=-1)


def gate_matrix(window, count):
    start = window[:, 0].astype(jnp.float32)
    span = (window[:, 1] - window[:, 0]).astype(jnp.float32)
    freqs = jnp.arange(count, dtype=jnp.float32)
    delta = freqs[:, None] - freqs[None, :]
    theta = 2.0 * math.pi * delta / NT
    safe = jnp.where(delta == 0.0, 1.0, jnp.sin(theta / 2.0))
    magnitude = jnp.where((delta == 0.0)[:, :, None], span[None, None, :] / NT,
                          jnp.sin(theta[:, :, None] * span[None, None, :] / 2.0) / (NT * safe[:, :, None]))
    phase = theta[:, :, None] * (start[None, None, :] + (span[None, None, :] - 1.0) / 2.0)
    return magnitude * jnp.cos(phase), magnitude * jnp.sin(phase)


def one_step(inputs):
    model, data, col_factors, row_factors, ranks, stepping = inputs
    f32 = jnp.float32
    vfac = col_factors.reshape(N_TILE, TPD, 2, RMAX, B).astype(f32)
    ufac = row_factors.reshape(N_TILE, TPD, 2, RMAX, B).astype(f32)
    slots = jnp.arange(TPD, dtype=jnp.int32)[None, :]
    offsets = slots - TPD // 2
    blocks = jnp.arange(N_TILE, dtype=jnp.int32)[:, None]
    target = blocks + offsets
    target_ok = (target >= 0) & (target < N_TILE)
    anchor = blocks - offsets
    anchor_ok = (anchor >= 0) & (anchor < N_TILE)
    target_c = jnp.clip(target, 0, N_TILE - 1).astype(jnp.int32)
    anchor_c = jnp.clip(anchor, 0, N_TILE - 1).astype(jnp.int32)
    levels = jnp.arange(RMAX, dtype=jnp.int32)
    xb = model.reshape(N_TILE, B, 2 * NV).astype(jnp.bfloat16).astype(f32)
    coef = jnp.einsum('csrb,cbv->csrv', vfac[:, :, 0], xb) + jnp.einsum('csrb,cbv->csrv', vfac[:, :, 1], rotate(xb))
    col_mask = (levels[None, None, :] < ranks[:, :, None]).astype(f32)
    coef = (coef * col_mask[..., None]).astype(jnp.bfloat16).astype(f32)
    received = coef[anchor_c, slots] * anchor_ok.astype(f32)[..., None, None]
    image = jnp.einsum('rskb,rskv->rbv', ufac[:, :, 0], received) + jnp.einsum('rskb,rskv->rbv', ufac[:, :, 1], rotate(received))
    resid = (image - data.reshape(N_TILE, B, 2 * NV).astype(f32)).astype(jnp.bfloat16).astype(f32)
    row_rank = jnp.where(anchor_ok, ranks[anchor_c, slots], 0)
    row_mask = (levels[None, None, :] < row_rank[:, :, None]).astype(f32)
    return_trip = jnp.einsum('rskb,rbv->rskv', ufac[:, :, 0], resid) - jnp.einsum('rskb,rbv->rskv', ufac[:, :, 1], rotate(resid))
    return_trip = (return_trip * row_mask[..., None]).astype(jnp.bfloat16).astype(f32)
    returned = return_trip[target_c, slots] * target_ok.astype(f32)[..., None, None]
    grad = jnp.einsum('csrb,csrv->cbv', vfac[:, :, 0], returned) - jnp.einsum('csrb,csrv->cbv', vfac[:, :, 1], rotate(returned))
    return model - stepping * grad.reshape(N_TILE * B, 2 * NV)


def reference(model_start, data, col_factors, row_factors, ranks, gate_window, step_sizes):
    count = model_start.shape[0]
    gate_re, gate_im = gate_matrix(gate_window, count)
    model = model_start
    for step in range(ITERS):
        moved = lax.map(one_step, (model, data, col_factors, row_factors, ranks, step_sizes))
        part_re = moved[..., :NV]
        part_im = moved[..., NV:]
        hp = lax.Precision.HIGHEST
        new_re = jnp.einsum('fgv,gnv->fnv', gate_re, part_re, precision=hp) - jnp.einsum('fgv,gnv->fnv', gate_im, part_im, precision=hp)
        new_im = jnp.einsum('fgv,gnv->fnv', gate_re, part_im, precision=hp) + jnp.einsum('fgv,gnv->fnv', gate_im, part_re, precision=hp)
        model = jnp.concatenate([new_re, new_im], axis=-1)
    return model
```

```python
import math

import jax
import jax.numpy as jnp
from jax import lax
from jax.experimental import pallas as pl
from jax.experimental.pallas import tpu as pltpu
from jax.sharding import PartitionSpec as P

NT = 2048
ITERS = 2
F32 = jnp.float32
BF16 = jnp.bfloat16


def slot_order(slots):
    center = slots // 2
    offsets = [s - center for s in range(slots)]
    key = {2: 0, 1: 1, 3: 2}
    far = sorted((o for o in offsets if o), key=lambda o: (key.get(abs(o), 3), abs(o), o))
    return far + [0]


def make_kernel(ntile, nfreq, slots, levels, rows, width):
    center = slots // 2
    half = width // 2
    order = slot_order(slots)

    def quarter_turn(sign):
        lane = lax.broadcasted_iota(jnp.int32, (1, width), 1)
        return jnp.where(lane < half, -sign, sign).astype(F32)

    def kernel(
        model_hbm, data_hbm, v_hbm, u_hbm, ranks, window, stepping,
        out,
        model_ref, data_ref, v, u, vt, ut, z_ref,
        fsent, fgot, asent, agot, zsent, zgot,
        local_sem, v_sem, u_sem, send_sem, recv_sem, zsend_sem, zrecv_sem,
    ):
        me = lax.axis_index("tile")
        freq = lax.axis_index("freq")

        def inside(index):
            return jnp.logical_and(index >= 0, index < ntile)

        load_model = pltpu.make_async_copy(model_hbm, model_ref, local_sem.at[0])
        load_data = pltpu.make_async_copy(data_hbm, data_ref, local_sem.at[1])
        load_v = [pltpu.make_async_copy(v_hbm.at[s], v.at[s], v_sem.at[s]) for s in range(slots)]
        load_u = [pltpu.make_async_copy(u_hbm.at[s], u.at[s], u_sem.at[s]) for s in range(slots)]
        load_model.start()
        for off in order:
            load_v[center + off].start()
        for off in order:
            load_u[center + off].start()
        load_data.start()

        barrier = pltpu.get_barrier_semaphore()
        expected = jnp.int32(nfreq - 1)
        for off in range(-center, center + 1):
            if off == 0:
                continue
            there = inside(me + off)

            @pl.when(there)
            def _():
                pl.semaphore_signal(barrier, inc=1, device_id={"tile": me + off})

            expected = expected + there.astype(jnp.int32)
        for other in range(1, nfreq):
            pl.semaphore_signal(barrier, inc=1, device_id={"freq": lax.rem(freq + other, nfreq)})

        for off in order:
            if off == 0:
                continue

            @pl.when(jnp.logical_not(inside(me - off)))
            def _():
                for step in range(ITERS):
                    fgot[step, center + off] = jnp.zeros((levels, width), BF16)

            @pl.when(jnp.logical_not(inside(me + off)))
            def _():
                for step in range(ITERS):
                    agot[step, center + off] = jnp.zeros((levels, width), BF16)

        plus = quarter_turn(1.0)
        minus = quarter_turn(-1.0)

        def rotated(value, sign_row):
            return (pltpu.roll(value, half, 1) * sign_row).astype(BF16)

        level_ids = lax.broadcasted_iota(jnp.int32, (levels, width), 0)

        def hop(src, dst, phase, step, s, target):
            return pltpu.make_async_remote_copy(
                src_ref=src.at[step, s], dst_ref=dst.at[step, s],
                send_sem=send_sem.at[step, phase, s], recv_sem=recv_sem.at[step, phase, s],
                device_id={"tile": target}, device_id_type=pl.DeviceIdType.MESH,
            )

        def freq_copy(step, other):
            return pltpu.make_async_remote_copy(
                src_ref=zsent.at[step], dst_ref=zgot.at[step, other - 1],
                send_sem=zsend_sem.at[step, other - 1], recv_sem=zrecv_sem.at[step, other - 1],
                device_id={"freq": lax.rem(freq + other, nfreq)},
                device_id_type=pl.DeviceIdType.MESH,
            )

        load_model.wait()
        model = model_ref[...]
        for step in range(ITERS):
            xb = model.astype(BF16)
            rx = rotated(xb.astype(F32), plus)
            for place, off in enumerate(order):
                s = center + off
                if step == 0:
                    load_v[s].wait()
                coef = jnp.dot(v[s, 0], xb, preferred_element_type=F32) + jnp.dot(
                    v[s, 1], rx, preferred_element_type=F32
                )
                coef = jnp.where(level_ids < ranks[me, s], coef, 0.0).astype(BF16)
                if off == 0:
                    fgot[step, s] = coef
                    continue
                fsent[step, s] = coef
                if step == 0 and place == 0:
                    pl.semaphore_wait(barrier, expected)

                @pl.when(inside(me + off))
                def _():
                    hop(fsent, fgot, 0, step, s, me + off).start()

            if step == 0:
                for off in order:
                    s = center + off
                    load_u[s].wait()
                    ut[s] = jnp.transpose(u[s].reshape(2 * levels, rows))
                load_data.wait()
            image = -data_ref[...].astype(F32)
            for off in [0] + order[:-1]:
                s = center + off
                if off != 0:

                    @pl.when(inside(me - off))
                    def _():
                        hop(fsent, fgot, 0, step, s, me).wait_recv()

                c = fgot[step, s]
                rc = rotated(c.astype(F32), plus)
                image = image + jnp.dot(
                    ut[s], jnp.concatenate([c, rc], axis=0), preferred_element_type=F32
                )
            resid = image.astype(BF16)
            rr = rotated(resid.astype(F32), minus)
            for off in order:
                s = center + off
                back = jnp.dot(u[s, 0], resid, preferred_element_type=F32) + jnp.dot(
                    u[s, 1], rr, preferred_element_type=F32
                )
                rank = ranks[jnp.clip(me - off, 0, ntile - 1), s]
                back = jnp.where(level_ids < rank, back, 0.0).astype(BF16)
                if off == 0:
                    agot[step, s] = back
                    continue
                asent[step, s] = back

                @pl.when(inside(me - off))
                def _():
                    hop(asent, agot, 1, step, s, me - off).start()

            if step == 0:
                for off in order:
                    s = center + off
                    vt[s] = jnp.transpose(v[s].reshape(2 * levels, rows))
                wf = window[...].astype(F32)
                ends = []
                for column in range(2):
                    wide = jnp.broadcast_to(wf[:, column:column + 1], (half, width))
                    wide = jnp.concatenate([wide, wide], axis=0)
                    ends.append(jnp.transpose(wide)[0:8])
                span = ends[1] - ends[0]
                own_gate = (span / NT)[0:1]
                gates = []
                for other in range(1, nfreq):
                    source = lax.rem(freq + nfreq - other, nfreq)
                    delta = (freq - source).astype(F32)
                    turn = delta * (ends[0] + ends[1] - 1.0)
                    turn = turn - (2 * NT) * jnp.floor(turn / (2 * NT))
                    phase = turn * (math.pi / NT)
                    theta = jnp.full_like(span, math.pi / NT) * delta
                    mag = jnp.sin(theta * span) / (NT * jnp.sin(theta))
                    gates.append(((mag * jnp.cos(phase))[0:1], (mag * jnp.sin(phase))[0:1] * plus))
            grad = jnp.zeros((rows, width), F32)
            for off in [0] + order[:-1]:
                s = center + off
                if off != 0:

                    @pl.when(inside(me + off))
                    def _():
                        hop(asent, agot, 1, step, s, me).wait_recv()

                b = agot[step, s]
                rb = rotated(b.astype(F32), minus)
                grad = grad + jnp.dot(
                    vt[s], jnp.concatenate([b, rb], axis=0), preferred_element_type=F32
                )
            z = model - stepping[0] * grad
            zsent[step] = z.astype(BF16)
            for other in range(1, nfreq):
                freq_copy(step, other).start()
            model = own_gate * z
            for other in range(1, nfreq):
                freq_copy(step, other).wait_recv()
                zg = zgot[step, other - 1].astype(F32)
                gre, gim = gates[other - 1]
                model = model + gre * zg + gim * pltpu.roll(zg, half, 1)
        out[...] = model

        for step in range(ITERS):
            for other in range(1, nfreq):
                freq_copy(step, other).wait_send()
            for off in order[:-1]:
                s = center + off

                @pl.when(inside(me + off))
                def _():
                    hop(fsent, fgot, 0, step, s, me).wait_send()

                @pl.when(inside(me - off))
                def _():
                    hop(asent, agot, 1, step, s, me).wait_send()

    return kernel


def on_device(model_start, data, col_factors, row_factors, ranks, gate_window, step_sizes):
    ntile = lax.axis_size("tile")
    nfreq = lax.axis_size("freq")
    slots, _, levels, rows = col_factors.shape[1:]
    width = model_start.shape[-1]
    any_space = pl.BlockSpec(memory_space=pl.ANY)
    vmem = pl.BlockSpec(memory_space=pltpu.VMEM)
    smem = pl.BlockSpec(memory_space=pltpu.SMEM)
    block = (ITERS, slots, levels, width)
    peers = max(nfreq - 1, 1)
    result = pl.pallas_call(
        make_kernel(ntile, nfreq, slots, levels, rows, width),
        name="gradient_steps",
        out_shape=jax.ShapeDtypeStruct((rows, width), F32),
        in_specs=[any_space, any_space, any_space, any_space, smem, vmem, smem],
        out_specs=vmem,
        scratch_shapes=[
            pltpu.VMEM((rows, width), F32),
            pltpu.VMEM((rows, width), BF16),
            pltpu.VMEM((slots, 2, levels, rows), BF16),
            pltpu.VMEM((slots, 2, levels, rows), BF16),
            pltpu.VMEM((slots, rows, 2 * levels), BF16),
            pltpu.VMEM((slots, rows, 2 * levels), BF16),
            pltpu.VMEM((rows, width), F32),
            pltpu.VMEM(block, BF16),
            pltpu.VMEM(block, BF16),
            pltpu.VMEM(block, BF16),
            pltpu.VMEM(block, BF16),
            pltpu.VMEM((ITERS, rows, width), BF16),
            pltpu.VMEM((ITERS, peers, rows, width), BF16),
            pltpu.SemaphoreType.DMA((2,)),
            pltpu.SemaphoreType.DMA((slots,)),
            pltpu.SemaphoreType.DMA((slots,)),
            pltpu.SemaphoreType.DMA((ITERS, 2, slots)),
            pltpu.SemaphoreType.DMA((ITERS, 2, slots)),
            pltpu.SemaphoreType.DMA((ITERS, peers)),
            pltpu.SemaphoreType.DMA((ITERS, peers)),
        ],
        compiler_params=pltpu.CompilerParams(collective_id=0, has_side_effects=True),
    )(model_start[0], data[0], col_factors[0], row_factors[0], ranks[0], gate_window, step_sizes)
    return result[None]


def solution(mesh):
    return jax.shard_map(
        on_device,
        mesh=mesh,
        in_specs=(
            P("freq", "tile", None),
            P("freq", "tile", None),
            P("freq", "tile", None, None, None),
            P("freq", "tile", None, None, None),
            P("freq", None, None),
            P(),
            P("freq"),
        ),
        out_specs=P("freq", "tile", None),
        check_vma=False,
    )
```

```python
import math

import jax
import jax.numpy as jnp
from jax import lax
from jax.experimental import pallas as pl
from jax.experimental.pallas import tpu as pltpu
from jax.sharding import PartitionSpec as P

NT = 2048
ITERS = 2
F32 = jnp.float32
BF16 = jnp.bfloat16
GROUPS = 4
ZPARTS = 2
RECEIVE = (0, 1, 2, 3)


def slot_order(slots):
    center = slots // 2
    offsets = [s - center for s in range(slots)]
    key = {2: 0, 3: 1, 1: 2}
    far = sorted((o for o in offsets if o), key=lambda o: (key.get(abs(o), 3), abs(o), -o))
    return far + [0]


def make_kernel(ntile, nfreq, slots, levels, rows, width):
    center = slots // 2
    half = width // 2
    order = slot_order(slots)
    per_group = slots // GROUPS
    groups = [list(range(g * per_group, (g + 1) * per_group)) for g in range(GROUPS)]
    group_rows = per_group * levels

    def kernel(
        model_hbm, data_hbm, v_hbm, u_hbm, ranks_hbm, window_hbm, stepping_hbm,
        out,
        ranks, window, stepping, model_ref, data_ref, v, u, vt, ut,
        fsent, fgot, asent, agot, zsent, zgot,
        local_sem, v_sem, u_sem, send_sem, recv_sem, zsend_sem, zrecv_sem,
    ):
        me = lax.axis_index("tile")
        freq = lax.axis_index("freq")

        def inside(index):
            return jnp.logical_and(index >= 0, index < ntile)

        def at(place):
            return pl.ds(place * levels, levels)

        def loads(hbm, ref, sem):
            return [
                pltpu.make_async_copy(
                    hbm.at[center + off, part],
                    ref.at[at(place), pl.ds(part * rows, rows)],
                    sem.at[place, part],
                )
                for place, off in enumerate(order)
                for part in range(2)
            ]

        load_model = pltpu.make_async_copy(model_hbm, model_ref, local_sem.at[0])
        load_data = pltpu.make_async_copy(data_hbm, data_ref, local_sem.at[1])
        load_ranks = pltpu.make_async_copy(ranks_hbm, ranks, local_sem.at[2])
        load_window = pltpu.make_async_copy(window_hbm, window, local_sem.at[3])
        load_step = pltpu.make_async_copy(stepping_hbm, stepping, local_sem.at[4])
        load_v = loads(v_hbm, v, v_sem)
        load_u = loads(u_hbm, u, u_sem)

        barrier = pltpu.get_barrier_semaphore()
        expected = jnp.int32(nfreq - 1)
        for off in range(-center, center + 1):
            if off == 0:
                continue
            there = inside(me + off)

            @pl.when(there)
            def _():
                pl.semaphore_signal(barrier, inc=1, device_id={"tile": me + off})

            expected = expected + there.astype(jnp.int32)
        for other in range(1, nfreq):
            pl.semaphore_signal(barrier, inc=1, device_id={"freq": lax.rem(freq + other, nfreq)})
        for copy in [load_model, load_ranks] + load_v + load_u + [load_data, load_window, load_step]:
            copy.start()

        for place, off in enumerate(order):
            if off == 0:
                continue

            @pl.when(jnp.logical_not(inside(me - off)))
            def _():
                for step in range(ITERS):
                    fgot[step, at(place)] = jnp.zeros((levels, width), BF16)

            @pl.when(jnp.logical_not(inside(me + off)))
            def _():
                for step in range(ITERS):
                    agot[step, at(place)] = jnp.zeros((levels, width), BF16)

        lane = lax.broadcasted_iota(jnp.int32, (1, width), 1)
        plus = jnp.where(lane < half, -1.0, 1.0).astype(F32)

        def turned(value):
            return pltpu.roll(value, half, 1) * plus

        level_ids = lax.broadcasted_iota(jnp.int32, (levels, width), 0)

        def hop(src, dst, phase, step, place, target):
            return pltpu.make_async_remote_copy(
                src_ref=src.at[step, at(place)], dst_ref=dst.at[step, at(place)],
                send_sem=send_sem.at[step, phase, place],
                recv_sem=recv_sem.at[step, phase, place],
                device_id={"tile": target}, device_id_type=pl.DeviceIdType.MESH,
            )

        def freq_copy(step, other, part):
            where = pl.ds(part * (rows // ZPARTS), rows // ZPARTS)
            return pltpu.make_async_remote_copy(
                src_ref=zsent.at[step, where], dst_ref=zgot.at[step, other - 1, where],
                send_sem=zsend_sem.at[step, other - 1, part],
                recv_sem=zrecv_sem.at[step, other - 1, part],
                device_id={"freq": lax.rem(freq + other, nfreq)},
                device_id_type=pl.DeviceIdType.MESH,
            )

        def spread(factor, values, sent, got, phase, step, heading, before):
            for g, places in enumerate(groups):
                before(g)
                block = jnp.dot(
                    factor[pl.ds(g * group_rows, group_rows)], values,
                    preferred_element_type=F32,
                )
                for index, place in enumerate(places):
                    off = order[place]
                    column = me if phase == 0 else jnp.clip(me - off, 0, ntile - 1)
                    part = block[index * levels:(index + 1) * levels]
                    part = jnp.where(level_ids < ranks[center + off, column], part, 0.0)
                    target = got if off == 0 else sent
                    target[step, at(place)] = part.astype(BF16)
                if phase == 0 and step == 0 and g == 0:
                    pl.semaphore_wait(barrier, expected)
                for place in places:
                    off = heading * order[place]
                    if off == 0:
                        continue

                    @pl.when(inside(me + off))
                    def _():
                        hop(sent, got, phase, step, place, me + off).start()

        def collect(turned_factor, sent, got, phase, step, heading, parts):
            size = rows // parts
            totals = [jnp.zeros((size, width), F32) for _ in range(2 * parts)]
            for g in RECEIVE:
                for place in groups[g]:
                    off = heading * order[place]
                    if off == 0:
                        continue

                    @pl.when(inside(me - off))
                    def _():
                        hop(sent, got, phase, step, place, me).wait_recv()

                values = got[step, pl.ds(g * group_rows, group_rows)]
                for part in range(parts):
                    for side in range(2):
                        start = side * rows + part * size
                        totals[2 * part + side] += jnp.dot(
                            turned_factor[g, pl.ds(start, size)], values,
                            preferred_element_type=F32,
                        )
                    if g == RECEIVE[-1]:
                        yield part, totals[2 * part], turned(totals[2 * part + 1])

        def no_wait(g):
            return None

        def wait_v(g):
            for place in groups[g]:
                for part in range(2):
                    load_v[2 * place + part].wait()

        load_model.wait()
        load_ranks.wait()
        model = model_ref[...]
        for step in range(ITERS):
            xb = model.astype(BF16)
            xx = jnp.concatenate([xb, turned(xb.astype(F32)).astype(BF16)], axis=0)
            spread(v, xx, fsent, fgot, 0, step, 1, wait_v if step == 0 else no_wait)
            if step == 0:
                for g, places in enumerate(groups):
                    for place in places:
                        for part in range(2):
                            load_u[2 * place + part].wait()
                    ut[g] = jnp.transpose(u[pl.ds(g * group_rows, group_rows)])
                load_data.wait()
            (_, direct, crossed), = collect(ut, fsent, fgot, 0, step, 1, 1)
            resid = (direct + crossed - data_ref[...].astype(F32)).astype(BF16)
            rr = jnp.concatenate([resid, (-turned(resid.astype(F32))).astype(BF16)], axis=0)
            spread(u, rr, asent, agot, 1, step, -1, no_wait)
            if step == 0:
                for g in range(GROUPS):
                    vt[g] = jnp.transpose(v[pl.ds(g * group_rows, group_rows)])
                load_window.wait()
                load_step.wait()
                wf = window[...].astype(F32)
                ends = [
                    jnp.broadcast_to(
                        jnp.concatenate([wf[row:row + 1]] * 2, axis=1), (8, width)
                    )
                    for row in range(2)
                ]
                span = ends[1] - ends[0]
                own_gate = (span / NT)[0:1]
                gates = []
                for other in range(1, nfreq):
                    source = lax.rem(freq + nfreq - other, nfreq)
                    delta = (freq - source).astype(F32)
                    turn = delta * (ends[0] + ends[1] - 1.0)
                    turn = turn - (2 * NT) * jnp.floor(turn / (2 * NT))
                    phase = turn * (math.pi / NT)
                    theta = jnp.full_like(span, math.pi / NT) * delta
                    mag = jnp.sin(theta * span) / (NT * jnp.sin(theta))
                    gates.append(((mag * jnp.cos(phase))[0:1], (mag * jnp.sin(phase))[0:1] * plus))
            size = rows // ZPARTS
            pieces = []
            for part, direct, crossed in collect(vt, asent, agot, 1, step, -1, ZPARTS):
                z = model[part * size:(part + 1) * size] - stepping[...] * (direct - crossed)
                zsent[step, pl.ds(part * size, size)] = z.astype(BF16)
                for other in range(1, nfreq):
                    freq_copy(step, other, part).start()
                pieces.append(own_gate * z)
            for part in range(ZPARTS):
                for other in range(1, nfreq):
                    freq_copy(step, other, part).wait_recv()
                    zg = zgot[step, other - 1, pl.ds(part * size, size)].astype(F32)
                    gre, gim = gates[other - 1]
                    pieces[part] += gre * zg + gim * pltpu.roll(zg, half, 1)
            model = jnp.concatenate(pieces, axis=0)
        out[...] = model

        for step in range(ITERS):
            for other in range(1, nfreq):
                for part in range(ZPARTS):
                    freq_copy(step, other, part).wait_send()
            for place, off in enumerate(order):
                if off == 0:
                    continue

                @pl.when(inside(me + off))
                def _():
                    hop(fsent, fgot, 0, step, place, me).wait_send()

                @pl.when(inside(me - off))
                def _():
                    hop(asent, agot, 1, step, place, me).wait_send()

    return kernel


def on_device(model_start, data, col_factors, row_factors, ranks, gate_window, step_sizes):
    ntile = lax.axis_size("tile")
    nfreq = lax.axis_size("freq")
    slots, _, levels, rows = col_factors.shape[1:]
    width = model_start.shape[-1]
    any_space = pl.BlockSpec(memory_space=pl.ANY)
    block = (ITERS, slots * levels, width)
    peers = max(nfreq - 1, 1)
    result = pl.pallas_call(
        make_kernel(ntile, nfreq, slots, levels, rows, width),
        name="gradient_steps",
        out_shape=pltpu.VMEM((rows, width), F32),
        in_specs=[any_space] * 7,
        out_specs=pl.BlockSpec(memory_space=pltpu.VMEM),
        scratch_shapes=[
            pltpu.SMEM((slots, ntile), jnp.int32),
            pltpu.VMEM((2, width // 2), jnp.int32),
            pltpu.VMEM((1, 1), F32),
            pltpu.VMEM((rows, width), F32),
            pltpu.VMEM((rows, width), BF16),
            pltpu.VMEM((slots * levels, 2 * rows), BF16),
            pltpu.VMEM((slots * levels, 2 * rows), BF16),
            pltpu.VMEM((GROUPS, 2 * rows, slots * levels // GROUPS), BF16),
            pltpu.VMEM((GROUPS, 2 * rows, slots * levels // GROUPS), BF16),
            pltpu.VMEM(block, BF16),
            pltpu.VMEM(block, BF16),
            pltpu.VMEM(block, BF16),
            pltpu.VMEM(block, BF16),
            pltpu.VMEM((ITERS, rows, width), BF16),
            pltpu.VMEM((ITERS, peers, rows, width), BF16),
            pltpu.SemaphoreType.DMA((5,)),
            pltpu.SemaphoreType.DMA((slots, 2)),
            pltpu.SemaphoreType.DMA((slots, 2)),
            pltpu.SemaphoreType.DMA((ITERS, 2, slots)),
            pltpu.SemaphoreType.DMA((ITERS, 2, slots)),
            pltpu.SemaphoreType.DMA((ITERS, peers, ZPARTS)),
            pltpu.SemaphoreType.DMA((ITERS, peers, ZPARTS)),
        ],
        compiler_params=pltpu.CompilerParams(collective_id=0, has_side_effects=True),
    )(
        model_start[0], data[0], col_factors[0], row_factors[0], ranks[0].T, gate_window.T,
        step_sizes.reshape(1, 1),
    )
    return result[None]


def solution(mesh):
    return jax.shard_map(
        on_device,
        mesh=mesh,
        in_specs=(
            P("freq", "tile", None),
            P("freq", "tile", None),
            P("freq", "tile", None, None, None),
            P("freq", "tile", None, None, None),
            P("freq", None, None),
            P(),
            P("freq"),
        ),
        out_specs=P("freq", "tile", None),
        check_vma=False,
    )
```

```python
import math

import jax
import jax.numpy as jnp
from jax import lax
from jax.experimental import pallas as pl
from jax.experimental.pallas import tpu as pltpu
from jax.sharding import PartitionSpec as P

NT = 2048
ITERS = 2
F32 = jnp.float32
BF16 = jnp.bfloat16
GROUPS = 4
ZPARTS = 2
RECEIVE = (0, 1)
MERGE = 2


def slot_order(slots):
    center = slots // 2
    offsets = [s - center for s in range(slots)]
    key = {2: 0, 3: 1, 1: 2}
    far = sorted((o for o in offsets if o), key=lambda o: (key.get(abs(o), 3), abs(o), -o))
    return far + [0]


def make_kernel(ntile, nfreq, slots, levels, rows, width):
    center = slots // 2
    half = width // 2
    order = slot_order(slots)
    per_group = slots // GROUPS
    groups = [list(range(g * per_group, (g + 1) * per_group)) for g in range(GROUPS)]
    group_rows = per_group * levels

    def kernel(
        model_hbm, data_hbm, v_hbm, u_hbm, ranks_hbm, window_hbm, stepping_hbm,
        out,
        ranks, window, stepping, model_ref, data_ref, v, u, vt, ut,
        fsent, fgot, asent, agot, zsent, zgot,
        local_sem, v_sem, u_sem, send_sem, recv_sem, zsend_sem, zrecv_sem,
    ):
        me = lax.axis_index("tile")
        freq = lax.axis_index("freq")

        def inside(index):
            return jnp.logical_and(index >= 0, index < ntile)

        def at(place):
            return pl.ds(place * levels, levels)

        def loads(hbm, ref, sem):
            return [
                pltpu.make_async_copy(
                    hbm.at[center + off, part],
                    ref.at[at(place), pl.ds(part * rows, rows)],
                    sem.at[place, part],
                )
                for place, off in enumerate(order)
                for part in range(2)
            ]

        load_model = pltpu.make_async_copy(model_hbm, model_ref, local_sem.at[0])
        load_data = pltpu.make_async_copy(data_hbm, data_ref, local_sem.at[1])
        load_ranks = pltpu.make_async_copy(ranks_hbm, ranks, local_sem.at[2])
        load_window = pltpu.make_async_copy(window_hbm, window, local_sem.at[3])
        load_step = pltpu.make_async_copy(stepping_hbm, stepping, local_sem.at[4])
        load_v = loads(v_hbm, v, v_sem)
        load_u = loads(u_hbm, u, u_sem)

        barrier = pltpu.get_barrier_semaphore()
        expected = jnp.int32(nfreq - 1)
        for off in range(-center, center + 1):
            if off == 0:
                continue
            there = inside(me + off)

            @pl.when(there)
            def _():
                pl.semaphore_signal(barrier, inc=1, device_id={"tile": me + off})

            expected = expected + there.astype(jnp.int32)
        for other in range(1, nfreq):
            pl.semaphore_signal(barrier, inc=1, device_id={"freq": lax.rem(freq + other, nfreq)})
        for copy in [load_model, load_ranks] + load_v + load_u + [load_data, load_window, load_step]:
            copy.start()

        for place, off in enumerate(order):
            if off == 0:
                continue

            @pl.when(jnp.logical_not(inside(me - off)))
            def _():
                for step in range(ITERS):
                    fgot[step, at(place)] = jnp.zeros((levels, width), BF16)

            @pl.when(jnp.logical_not(inside(me + off)))
            def _():
                for step in range(ITERS):
                    agot[step, at(place)] = jnp.zeros((levels, width), BF16)

        lane = lax.broadcasted_iota(jnp.int32, (1, width), 1)
        plus = jnp.where(lane < half, -1.0, 1.0).astype(F32)

        def turned(value):
            return pltpu.roll(value, half, 1) * plus

        level_ids = lax.broadcasted_iota(jnp.int32, (levels, width), 0)

        def hop(src, dst, phase, step, place, target):
            return pltpu.make_async_remote_copy(
                src_ref=src.at[step, at(place)], dst_ref=dst.at[step, at(place)],
                send_sem=send_sem.at[step, phase, place],
                recv_sem=recv_sem.at[step, phase, place],
                device_id={"tile": target}, device_id_type=pl.DeviceIdType.MESH,
            )

        def freq_copy(step, other, part):
            where = pl.ds(part * (rows // ZPARTS), rows // ZPARTS)
            return pltpu.make_async_remote_copy(
                src_ref=zsent.at[step, where], dst_ref=zgot.at[step, other - 1, where],
                send_sem=zsend_sem.at[step, other - 1, part],
                recv_sem=zrecv_sem.at[step, other - 1, part],
                device_id={"freq": lax.rem(freq + other, nfreq)},
                device_id_type=pl.DeviceIdType.MESH,
            )

        def spread(factor, values, sent, got, phase, step, heading, before):
            for g, places in enumerate(groups):
                before(g)
                block = jnp.dot(
                    factor[pl.ds(g * group_rows, group_rows)], values,
                    preferred_element_type=F32,
                )
                for index, place in enumerate(places):
                    off = order[place]
                    column = me if phase == 0 else jnp.clip(me - off, 0, ntile - 1)
                    part = block[index * levels:(index + 1) * levels]
                    part = jnp.where(level_ids < ranks[center + off, column], part, 0.0)
                    target = got if off == 0 else sent
                    target[step, at(place)] = part.astype(BF16)
                if phase == 0 and step == 0 and g == 0:
                    pl.semaphore_wait(barrier, expected)
                for place in places:
                    off = heading * order[place]
                    if off == 0:
                        continue

                    @pl.when(inside(me + off))
                    def _():
                        hop(sent, got, phase, step, place, me + off).start()

        def collect(turned_factor, sent, got, phase, step, heading, parts):
            size = rows // parts
            totals = [jnp.zeros((size, width), F32) for _ in range(2 * parts)]
            for g in RECEIVE:
                for place in [p for m in range(MERGE) for p in groups[g * MERGE + m]]:
                    off = heading * order[place]
                    if off == 0:
                        continue

                    @pl.when(inside(me - off))
                    def _():
                        hop(sent, got, phase, step, place, me).wait_recv()

                values = got[step, pl.ds(g * MERGE * group_rows, MERGE * group_rows)]
                for part in range(parts):
                    for side in range(2):
                        start = side * rows + part * size
                        totals[2 * part + side] += jnp.dot(
                            turned_factor[g, pl.ds(start, size)], values,
                            preferred_element_type=F32,
                        )
                    if g == RECEIVE[-1]:
                        yield part, totals[2 * part], turned(totals[2 * part + 1])

        def no_wait(g):
            return None

        def wait_v(g):
            for place in groups[g]:
                for part in range(2):
                    load_v[2 * place + part].wait()

        load_model.wait()
        load_ranks.wait()
        model = model_ref[...]
        for step in range(ITERS):
            xb = model.astype(BF16)
            xx = jnp.concatenate([xb, turned(xb.astype(F32)).astype(BF16)], axis=0)
            spread(v, xx, fsent, fgot, 0, step, 1, wait_v if step == 0 else no_wait)
            if step == 0:
                for g, places in enumerate(groups):
                    for place in places:
                        for part in range(2):
                            load_u[2 * place + part].wait()
                    ut[g // MERGE, :, (g % MERGE) * group_rows:(g % MERGE + 1) * group_rows] = jnp.transpose(u[pl.ds(g * group_rows, group_rows)])
                load_data.wait()
            (_, direct, crossed), = collect(ut, fsent, fgot, 0, step, 1, 1)
            resid = (direct + crossed - data_ref[...].astype(F32)).astype(BF16)
            rr = jnp.concatenate([resid, (-turned(resid.astype(F32))).astype(BF16)], axis=0)
            spread(u, rr, asent, agot, 1, step, -1, no_wait)
            if step == 0:
                for g in range(GROUPS):
                    vt[g // MERGE, :, (g % MERGE) * group_rows:(g % MERGE + 1) * group_rows] = jnp.transpose(v[pl.ds(g * group_rows, group_rows)])
                load_window.wait()
                load_step.wait()
                wf = window[...].astype(F32)
                ends = [
                    jnp.broadcast_to(
                        jnp.concatenate([wf[row:row + 1]] * 2, axis=1), (8, width)
                    )
                    for row in range(2)
                ]
                span = ends[1] - ends[0]
                own_gate = (span / NT)[0:1]
                gates = []
                for other in range(1, nfreq):
                    source = lax.rem(freq + nfreq - other, nfreq)
                    delta = (freq - source).astype(F32)
                    turn = delta * (ends[0] + ends[1] - 1.0)
                    turn = turn - (2 * NT) * jnp.floor(turn / (2 * NT))
                    phase = turn * (math.pi / NT)
                    theta = jnp.full_like(span, math.pi / NT) * delta
                    mag = jnp.sin(theta * span) / (NT * jnp.sin(theta))
                    gates.append(((mag * jnp.cos(phase))[0:1], (mag * jnp.sin(phase))[0:1] * plus))
            size = rows // ZPARTS
            pieces = []
            for part, direct, crossed in collect(vt, asent, agot, 1, step, -1, ZPARTS):
                z = model[part * size:(part + 1) * size] - stepping[...] * (direct - crossed)
                zsent[step, pl.ds(part * size, size)] = z.astype(BF16)
                for other in range(1, nfreq):
                    freq_copy(step, other, part).start()
                pieces.append(own_gate * z)
            for part in range(ZPARTS):
                for other in range(1, nfreq):
                    freq_copy(step, other, part).wait_recv()
                    zg = zgot[step, other - 1, pl.ds(part * size, size)].astype(F32)
                    gre, gim = gates[other - 1]
                    pieces[part] += gre * zg + gim * pltpu.roll(zg, half, 1)
            model = jnp.concatenate(pieces, axis=0)
        out[...] = model

        for step in range(ITERS):
            for other in range(1, nfreq):
                for part in range(ZPARTS):
                    freq_copy(step, other, part).wait_send()
            for place, off in enumerate(order):
                if off == 0:
                    continue

                @pl.when(inside(me + off))
                def _():
                    hop(fsent, fgot, 0, step, place, me).wait_send()

                @pl.when(inside(me - off))
                def _():
                    hop(asent, agot, 1, step, place, me).wait_send()

    return kernel


def on_device(model_start, data, col_factors, row_factors, ranks, gate_window, step_sizes):
    ntile = lax.axis_size("tile")
    nfreq = lax.axis_size("freq")
    slots, _, levels, rows = col_factors.shape[1:]
    width = model_start.shape[-1]
    any_space = pl.BlockSpec(memory_space=pl.ANY)
    block = (ITERS, slots * levels, width)
    peers = max(nfreq - 1, 1)
    result = pl.pallas_call(
        make_kernel(ntile, nfreq, slots, levels, rows, width),
        name="gradient_steps",
        out_shape=pltpu.VMEM((rows, width), F32),
        in_specs=[any_space] * 7,
        out_specs=pl.BlockSpec(memory_space=pltpu.VMEM),
        scratch_shapes=[
            pltpu.SMEM((slots, ntile), jnp.int32),
            pltpu.VMEM((2, width // 2), jnp.int32),
            pltpu.VMEM((1, 1), F32),
            pltpu.VMEM((rows, width), F32),
            pltpu.VMEM((rows, width), BF16),
            pltpu.VMEM((slots * levels, 2 * rows), BF16),
            pltpu.VMEM((slots * levels, 2 * rows), BF16),
            pltpu.VMEM((GROUPS // MERGE, 2 * rows, slots * levels // GROUPS * MERGE), BF16),
            pltpu.VMEM((GROUPS // MERGE, 2 * rows, slots * levels // GROUPS * MERGE), BF16),
            pltpu.VMEM(block, BF16),
            pltpu.VMEM(block, BF16),
            pltpu.VMEM(block, BF16),
            pltpu.VMEM(block, BF16),
            pltpu.VMEM((ITERS, rows, width), BF16),
            pltpu.VMEM((ITERS, peers, rows, width), BF16),
            pltpu.SemaphoreType.DMA((5,)),
            pltpu.SemaphoreType.DMA((slots, 2)),
            pltpu.SemaphoreType.DMA((slots, 2)),
            pltpu.SemaphoreType.DMA((ITERS, 2, slots)),
            pltpu.SemaphoreType.DMA((ITERS, 2, slots)),
            pltpu.SemaphoreType.DMA((ITERS, peers, ZPARTS)),
            pltpu.SemaphoreType.DMA((ITERS, peers, ZPARTS)),
        ],
        compiler_params=pltpu.CompilerParams(collective_id=0, has_side_effects=True),
    )(
        model_start[0], data[0], col_factors[0], row_factors[0], ranks[0].T, gate_window.T,
        step_sizes.reshape(1, 1),
    )
    return result[None]


def solution(mesh):
    return jax.shard_map(
        on_device,
        mesh=mesh,
        in_specs=(
            P("freq", "tile", None),
            P("freq", "tile", None),
            P("freq", "tile", None, None, None),
            P("freq", "tile", None, None, None),
            P("freq", None, None),
            P(),
            P("freq"),
        ),
        out_specs=P("freq", "tile", None),
        check_vma=False,
    )
```
